32 devices in a mesh: row: 8 (over z, y), col: 4 (over x, core).
Axes of the slice: x: 2, y: 2, z: 4, core: 2. Of those that a mesh axis runs over, the one named last changes fastest.
Arguments:
- front: float32 [12, 8, 128, 24, 4, 128], P(None, 'row', None, None, 'col'), may hold values from -2.01 to 16, as said below
- child_updates: float32 [12, 8, 128, 12, 4, 128], P(None, 'row', None, None, 'col'), may hold values from -0.5 to 0.005, as said below
- child_maps: int32 [2, 48], replicated, may hold values from 0 to 62, as said below
- child_orders: int32 [2], replicated, may hold values from 6017 to 6144, as said below
Outputs:
- factored: float32 [12, 8, 128, 24, 4, 128], P(None, 'row', None, None, 'col')
The draws below stay inside these ranges and needn't reach their ends.
Inputs may be any that keep to these rules, and one draw needn't show every extreme that they name: `front`: symmetric; with the children's updates added as above it is positive definite. `child_updates`: each child's update is symmetric. `child_maps`: each child's map adds to a tile's index an offset that is the same over aligned runs of 8 child tiles, rises strictly from run to run, is 0 on the first run and 15 on the last, and differs modulo 8 between runs. `child_orders`: each order lies in the last tile of its padded update; one of the two is 6144.
All inputs are finite; a program needn't handle non-finite values.
Results may differ from the reference program's by a relative error of at most 0.00005.
Values sent between devices are 32-bit elements; how exact they have to be, the bound alone decides.
A program may use at most 128 MiB of HBM per device.

```python
import math
import jax
import jax.numpy as jnp
from jax import lax

TILE = 128
FT = 96
CT = 48
PT = 5
PANELS = 1
RUN = 8
N_ROW = 8
N_COL = 4


def shift_down(values, count):
    return jnp.concatenate([jnp.zeros((count,), jnp.float32), values[:-count]])


def draw_front(key, part):
    front_order = FT * TILE
    layers = front_order // 256
    perm_key, weight_key, shift_key, fill_key = jax.random.split(key, 4)
    cells = jax.random.permutation(perm_key, front_order).astype(jnp.int32)
    weights = jnp.exp(jax.random.uniform(weight_key, (3, front_order), jnp.float32, math.log(0.4), math.log(2.0)))
    shifts = jax.random.uniform(shift_key, (front_order,), jnp.float32, 2.0, 3.0)
    fill = jax.random.uniform(fill_key, (front_order, front_order), jnp.float32, -0.001, 0.001)
    grid_cells = jnp.arange(front_order, dtype=jnp.int32)
    along_x = jnp.where(grid_cells // 256 < layers - 1, weights[0], 0.0).astype(jnp.float32)
    along_y = jnp.where(grid_cells // 16 % 16 < 15, weights[1], 0.0).astype(jnp.float32)
    along_z = jnp.where(grid_cells % 16 < 15, weights[2], 0.0).astype(jnp.float32)
    degree = along_x + along_y + along_z + shift_down(along_x, 256) + shift_down(along_y, 16) + shift_down(along_z, 1)
    index_x = along_x[cells]
    index_y = along_y[cells]
    index_z = along_z[cells]
    row_cells = cells[:, None]
    col_cells = cells[None, :]
    first = row_cells < col_cells
    gap = jnp.abs(row_cells - col_cells)

    def pick(values):
        return jnp.where(first, values[:, None], values[None, :])
    edge = jnp.where(gap == 256, pick(index_x), jnp.where(gap == 16, pick(index_y), jnp.where(gap == 1, pick(index_z), 0.0)))
    symmetric_fill = 0.5 * (fill + fill.T)
    pivots = degree[cells] + shifts
    full_matrix = jnp.where(gap == 0, pivots[:, None], symmetric_fill - edge)
    return full_matrix.reshape(FT // N_ROW, N_ROW, TILE, FT // N_COL, N_COL, TILE)


def draw_child_updates(key, part):
    child_order = CT * TILE
    half_rows = N_ROW // 2
    limit = 0.005
    diagonal = jnp.arange(child_order)[:, None] == jnp.arange(child_order)[None, :]
    blocks = []
    for child in range(2):
        child_key = jax.random.fold_in(key, 17 + child)
        entry_key, pivot_key = jax.random.split(child_key)
        entries = jax.random.uniform(entry_key, (child_order, child_order), jnp.float32, -limit, limit)
        pivots = jax.random.uniform(pivot_key, (child_order,), jnp.float32, -0.5, -0.15)
        symmetric = 0.5 * (entries + entries.T)
        full_matrix = jnp.where(diagonal, pivots[:, None], symmetric)
        blocks.append(full_matrix.reshape(CT // half_rows, half_rows, TILE, CT // N_COL, N_COL, TILE))
    return jnp.stack(blocks, 1).reshape(CT // half_rows, N_ROW, TILE, CT // N_COL, N_COL, TILE)


def draw_child_maps(key, part):
    run_count = CT // RUN
    middle = run_count - 2
    halfway = N_COL // 2
    tile_index = jnp.arange(CT, dtype=jnp.int32)
    first_key, second_key = jax.random.split(jax.random.fold_in(key, 31))
    residues = jax.random.permutation(first_key, 6)[:middle].astype(jnp.int32) + 1
    lifted = residues + 8 * jax.random.randint(second_key, (middle,), 0, 2).astype(jnp.int32)
    offsets_first = jnp.concatenate([jnp.zeros((1,), jnp.int32), jnp.sort(lifted), jnp.full((1,), 15, jnp.int32)])
    third_key, fourth_key = jax.random.split(jax.random.fold_in(key, 32))
    others = jnp.array([value for value in range(2, 7) if value != halfway], jnp.int32)
    picked = jax.random.permutation(third_key, others)[:middle - 2].astype(jnp.int32)
    chosen = jnp.concatenate([jnp.full((1,), halfway, jnp.int32), picked])
    raised = chosen + 8 * jax.random.randint(fourth_key, (middle - 1,), 0, 2).astype(jnp.int32)
    offsets_second = jnp.concatenate([jnp.zeros((1,), jnp.int32), jnp.ones((1,), jnp.int32), jnp.sort(raised), jnp.full((1,), 15, jnp.int32)])
    first_map = tile_index + offsets_first[tile_index // RUN]
    second_map = tile_index + offsets_second[tile_index // RUN]
    return jnp.stack([first_map, second_map]).astype(jnp.int32)


def draw_child_orders(key, part):
    first_key, second_key = jax.random.split(key)
    shortfall = jax.random.randint(first_key, (2,), 0, TILE).astype(jnp.int32)
    full_child = jax.random.randint(second_key, (), 0, 2).astype(jnp.int32)
    shortfall = jnp.where(jnp.arange(2, dtype=jnp.int32) == full_child, 0, shortfall)
    return (CT * TILE - shortfall).astype(jnp.int32)


def setup_inputs(seed: int = 0) -> dict:
    streams_of = jax.random.split(jax.random.key(seed), 5)
    front = draw_front(jax.random.fold_in(streams_of[4], 71), 0)
    child_updates = draw_child_updates(jax.random.fold_in(streams_of[4], 71), 0)
    child_maps = draw_child_maps(jax.random.fold_in(streams_of[4], 71), 0)
    child_orders = draw_child_orders(jax.random.fold_in(streams_of[4], 71), 0)
    return dict(front=front, child_updates=child_updates, child_maps=child_maps, child_orders=child_orders)


def reference(front, child_updates, child_maps, child_orders):
    front_order = FT * TILE
    child_order = CT * TILE
    half_rows = N_ROW // 2
    leading_order = PANELS * PT * TILE
    front_tiles = front.reshape(FT, TILE, FT, TILE).transpose(0, 2, 1, 3)
    children = child_updates.reshape(CT // half_rows, 2, half_rows, TILE, CT // N_COL, N_COL, TILE)
    positions = jnp.arange(child_order, dtype=jnp.int32)
    for child in range(2):
        update = children[:, child].reshape(child_order, child_order)
        inside = (positions < child_orders[child]).astype(jnp.float32)
        update = update * inside[:, None] * inside[None, :]
        update_tiles = update.reshape(CT, TILE, CT, TILE).transpose(0, 2, 1, 3)
        mapping = child_maps[child].astype(jnp.int32)
        front_tiles = front_tiles.at[mapping[:, None], mapping[None, :]].add(update_tiles)
    assembled = front_tiles.transpose(0, 2, 1, 3).reshape(front_order, front_order)
    leading = jnp.tril(jnp.linalg.cholesky(assembled[:leading_order, :leading_order]))
    lower_left = lax.linalg.triangular_solve(leading, assembled[leading_order:, :leading_order], left_side=False, lower=True, transpose_a=True)
    schur = assembled[leading_order:, leading_order:] - jnp.dot(lower_left.astype(jnp.float32), lower_left.T.astype(jnp.float32), precision=lax.Precision.HIGHEST, preferred_element_type=jnp.float32)
    upper_rows = jnp.concatenate([leading, jnp.zeros((leading_order, front_order - leading_order), jnp.float32)], axis=1)
    lower_rows = jnp.concatenate([lower_left, schur], axis=1)
    factored = jnp.concatenate([upper_rows, lower_rows], axis=0)
    return factored.reshape(front.shape)
```

```python
import jax
import jax.numpy as jnp
from jax import lax
from jax.sharding import PartitionSpec as P

PT = 5
PANELS = 1
RUN = 8


highest = lax.Precision.HIGHEST


def earlier_equal(values):
    length = values.shape[-1]
    matches = values[..., :, None] == values[..., None, :]
    earlier = jnp.arange(length)[None, :] < jnp.arange(length)[:, None]
    return jnp.sum(jnp.logical_and(matches, earlier), axis=-1)


def one_hot(values, length):
    return (values[..., None] == jnp.arange(length, dtype=jnp.int32)).astype(jnp.float32)


def shards(front, child_updates, child_maps, child_orders):
    row_tiles, tile_size, col_tiles = (front.shape[0], front.shape[2], front.shape[3])
    child_rows, child_cols = (child_updates.shape[0], child_updates.shape[3])
    rows_count = lax.axis_size("row")
    cols_count = lax.axis_size("col")
    half_rows = rows_count // 2
    row_id = lax.axis_index("row")
    col_id = lax.axis_index("col")
    matrix = front.reshape(row_tiles, tile_size, col_tiles, tile_size)
    pieces = child_updates.reshape(child_rows, tile_size, child_cols, tile_size)
    cap_rows = max(1, 2 * RUN // rows_count)
    cap_cols = max(1, RUN // cols_count) ** 2
    sources = jnp.arange(rows_count, dtype=jnp.int32)
    source_child = sources // half_rows
    source_maps = jnp.where(
        source_child[:, None] == 0, child_maps[0][None, :], child_maps[1][None, :]
    )
    child_row_index = (
        jnp.arange(child_rows, dtype=jnp.int32)[None, :] * half_rows
        + (sources % half_rows)[:, None]
    )
    mapped_rows = jnp.take_along_axis(source_maps, child_row_index, axis=1)
    dest_rows = mapped_rows % rows_count
    slot_rows = mapped_rows // rows_count
    child_col_index = (
        jnp.arange(child_cols, dtype=jnp.int32)[None, :] * cols_count
        + jnp.arange(cols_count, dtype=jnp.int32)[:, None]
    )
    mapped_cols = child_maps[:, child_col_index]
    dest_cols = mapped_cols % cols_count
    slot_cols = mapped_cols // cols_count
    my_child = row_id // half_rows
    my_order = jnp.where(my_child == 0, child_orders[0], child_orders[1])
    my_rows = child_row_index[row_id]
    my_cols = jnp.arange(child_cols, dtype=jnp.int32) * cols_count + col_id
    offsets = jnp.arange(tile_size, dtype=jnp.int32)[None, :]
    row_keep = (my_rows[:, None] * tile_size + offsets < my_order).astype(jnp.float32)
    col_keep = (my_cols[:, None] * tile_size + offsets < my_order).astype(jnp.float32)
    pieces = pieces * row_keep[:, :, None, None] * col_keep[None, None, :, :]
    capacity = cap_rows * cap_cols
    tile_count = child_rows * child_cols
    source_dest_cols = dest_cols[source_child]
    source_slot_cols = slot_cols[source_child]
    tile_dest = (
        dest_rows[:, None, :, None] * cols_count + source_dest_cols[:, :, None, :]
    ).reshape(rows_count, cols_count, tile_count)
    rank_tiles = earlier_equal(tile_dest)
    send_tiles = (
        one_hot(tile_dest[row_id, col_id], rows_count * cols_count)[:, :, None]
        * one_hot(rank_tiles[row_id, col_id], capacity)[:, None, :]
    )
    flat_pieces = pieces.transpose(0, 2, 1, 3).reshape(tile_count, tile_size, tile_size)
    outgoing = jnp.einsum("fpq,frs->pqrs", send_tiles, flat_pieces, precision=highest)
    incoming = lax.all_to_all(outgoing, ("row", "col"), split_axis=0, concat_axis=0, tiled=True)
    arrive_tiles = (tile_dest == row_id * cols_count + col_id).astype(jnp.float32)
    row_slot_flat = jnp.broadcast_to(
        slot_rows[:, None, :, None], (rows_count, cols_count, child_rows, child_cols)
    ).reshape(rows_count, cols_count, tile_count)
    col_slot_flat = jnp.broadcast_to(
        source_slot_cols[:, :, None, :], (rows_count, cols_count, child_rows, child_cols)
    ).reshape(rows_count, cols_count, tile_count)
    placement = jnp.einsum(
        "jlf,jlfa,jlfb,jlfq->abjlq",
        arrive_tiles,
        one_hot(row_slot_flat, row_tiles),
        one_hot(col_slot_flat, col_tiles),
        one_hot(rank_tiles, capacity),
        precision=highest,
    )
    placement = placement.reshape(row_tiles, col_tiles, rows_count * cols_count, capacity)
    added = jnp.einsum("abpq,pqrs->arbs", placement, incoming, precision=highest)
    matrix = matrix + added
    glob_rows = jnp.arange(row_tiles, dtype=jnp.int32) * rows_count + row_id

    panel_tiles = PANELS * PT
    panel_order = panel_tiles * tile_size
    lead_cols = -(-panel_tiles // cols_count)
    high = lax.Precision.HIGH
    panel_rows = lax.all_gather(matrix[:, :, :lead_cols, :], "col", axis=3)
    panel_rows = panel_rows.reshape(row_tiles * tile_size, lead_cols * cols_count * tile_size)
    panel_rows = panel_rows[:, :panel_order]
    leading = lax.all_gather(panel_rows[:tile_size], "row", axis=0)[:panel_tiles]
    leading = leading.reshape(panel_order, panel_order)
    panel_cols = lax.all_gather(matrix[0], "row", axis=0)[:panel_tiles]
    panel_cols = panel_cols.reshape(panel_order, col_tiles * tile_size)
    factor = jnp.tril(jnp.linalg.cholesky(leading))
    inverse = lax.linalg.triangular_solve(
        factor, jnp.eye(panel_order, dtype=jnp.float32), left_side=True, lower=True
    )
    lower_rows = jnp.einsum("rx,yx->ry", panel_rows, inverse, precision=high)
    lower_cols = jnp.einsum("yx,xc->yc", inverse, panel_cols, precision=high)
    below = (glob_rows >= panel_tiles)[:, None, None]
    lower_tiles = jnp.where(below, lower_rows.reshape(row_tiles, tile_size, panel_order), 0.0)
    update = jnp.einsum(
        "trx,xus->trus",
        lower_tiles,
        lower_cols.reshape(panel_order, col_tiles, tile_size),
        precision=high,
    )
    matrix = jnp.where(below[..., None], matrix - update, 0.0)
    factor_row = lax.dynamic_slice_in_dim(
        factor, jnp.minimum(row_id, panel_tiles - 1) * tile_size, tile_size, 0
    )
    top = jnp.where(row_id < panel_tiles, factor_row, lower_tiles[0])
    panel = jnp.concatenate([top[None], lower_tiles[1:]], 0)
    for local_col in range(lead_cols):
        column = local_col * cols_count + col_id
        piece = lax.dynamic_slice_in_dim(
            panel, jnp.minimum(column, panel_tiles - 1) * tile_size, tile_size, 2
        )
        matrix = matrix.at[:, :, local_col, :].set(
            jnp.where(column < panel_tiles, piece, matrix[:, :, local_col, :])
        )
    return matrix.reshape(row_tiles, 1, tile_size, col_tiles, 1, tile_size)


def solution(mesh):
    in_specs = (
        P(None, "row", None, None, "col", None),
        P(None, "row", None, None, "col", None),
        P(),
        P(),
    )
    out_specs = P(None, "row", None, None, "col", None)
    return jax.shard_map(shards, mesh=mesh, in_specs=in_specs, out_specs=out_specs, check_vma=False)
```

```python
import functools
import jax
import jax.numpy as jnp
from jax import lax
from jax.experimental import pallas as pl
from jax.experimental.pallas import tpu as pltpu
from jax.sharding import PartitionSpec as P

PT = 5
PANELS = 1
RUN = 8


highest = lax.Precision.HIGHEST


def earlier_equal(values):
    length = values.shape[-1]
    matches = values[..., :, None] == values[..., None, :]
    earlier = jnp.arange(length)[None, :] < jnp.arange(length)[:, None]
    return jnp.sum(jnp.logical_and(matches, earlier), axis=-1)


def one_hot(values, length):
    return (values[..., None] == jnp.arange(length, dtype=jnp.int32)).astype(jnp.float32)


def split(value, axis, second):
    rounded = lax.reduce_precision(value, 8, 7)
    large = rounded.astype(jnp.bfloat16)
    small = (value - rounded).astype(jnp.bfloat16)
    return jnp.concatenate([large, small, large] if second else [large, large, small], axis)


def update_kernel(panel_tiles, rows_count, cols_count, ids, m_ref, l_ref, c_ref, p_ref, o_ref):
    block, tile_size, col_tiles, _ = m_ref.shape
    lead_cols = p_ref.shape[0]
    lhs = l_ref[...].reshape(block * tile_size, l_ref.shape[2])
    local = lax.broadcasted_iota(jnp.int32, (block, tile_size, tile_size), 0)
    glob = (local + pl.program_id(0) * block) * rows_count + ids[0]
    for pair in range(col_tiles // 2):
        product = jnp.dot(
            lhs,
            c_ref[:, pair * 2 * tile_size : (pair + 1) * 2 * tile_size],
            preferred_element_type=jnp.float32,
        )
        for half in range(2):
            column = 2 * pair + half
            part = product[:, half * tile_size : (half + 1) * tile_size]
            tiles = m_ref[:, :, column, :] - part.reshape(block, tile_size, tile_size)
            tiles = jnp.where(glob >= panel_tiles, tiles, 0.0)
            if column < lead_cols:
                inside = column * cols_count + ids[1] < panel_tiles
                tiles = jnp.where(inside, p_ref[column], tiles)
            o_ref[:, :, column, :] = tiles


def update(ids, matrix, lower_tiles, lower_cols, panel, panel_tiles, rows_count, cols_count):
    row_tiles, tile_size, col_tiles, _ = matrix.shape
    depth = lower_tiles.shape[2]
    block = next(size for size in (4, 3, 2, 1) if row_tiles % size == 0)
    matrix_spec = pl.BlockSpec((block, tile_size, col_tiles, tile_size), lambda i: (i, 0, 0, 0))
    return pl.pallas_call(
        functools.partial(update_kernel, panel_tiles, rows_count, cols_count),
        grid=(row_tiles // block,),
        in_specs=[
            pl.BlockSpec(memory_space=pltpu.SMEM),
            matrix_spec,
            pl.BlockSpec((block, tile_size, depth), lambda i: (i, 0, 0)),
            pl.BlockSpec(lower_cols.shape, lambda i: (0, 0), pipeline_mode=pl.Buffered(1)),
            pl.BlockSpec((panel.shape[0], block, tile_size, tile_size), lambda i: (0, i, 0, 0)),
        ],
        out_specs=matrix_spec,
        out_shape=jax.ShapeDtypeStruct(matrix.shape, jnp.float32),
        compiler_params=pltpu.CompilerParams(vmem_limit_bytes=60 * 1024 * 1024),
    )(ids, matrix, lower_tiles, lower_cols, panel)


def shards(front, child_updates, child_maps, child_orders):
    row_tiles, tile_size, col_tiles = (front.shape[0], front.shape[2], front.shape[3])
    child_rows, child_cols = (child_updates.shape[0], child_updates.shape[3])
    rows_count = lax.axis_size("row")
    cols_count = lax.axis_size("col")
    half_rows = rows_count // 2
    row_id = lax.axis_index("row")
    col_id = lax.axis_index("col")
    matrix = front.reshape(row_tiles, tile_size, col_tiles, tile_size)
    pieces = child_updates.reshape(child_rows, tile_size, child_cols, tile_size)
    panel_tiles = PANELS * PT
    panel_order = panel_tiles * tile_size
    lead_cols = -(-panel_tiles // cols_count)
    high = lax.Precision.HIGH
    panel_range = jnp.arange(panel_tiles, dtype=jnp.int32)

    def place_row(tile_row, tiles):
        return jnp.where((panel_range == tile_row)[:, None, None, None], tiles[None], 0.0)

    lead = place_row(row_id, matrix[0, :, :lead_cols, :])
    for index in range(-(-panel_tiles // half_rows)):
        child_row = index * half_rows + row_id % half_rows
        lead = lead + place_row(child_row, pieces[index, :, :lead_cols, :])
    col_range = jnp.arange(cols_count, dtype=jnp.int32)
    lead = jnp.where((col_range == col_id)[:, None], lead[:, :, :, None, :], 0.0)
    lead = lead.reshape(panel_order, lead_cols * cols_count * tile_size)[:, :panel_order]
    leading = lax.psum(lead, ("row", "col"))
    factor = jnp.tril(jnp.linalg.cholesky(leading))
    inverse = lax.linalg.triangular_solve(
        factor, jnp.eye(panel_order, dtype=jnp.float32), left_side=True, lower=True
    )
    cap_rows = max(1, 2 * RUN // rows_count)
    cap_cols = max(1, RUN // cols_count) ** 2
    sources = jnp.arange(rows_count, dtype=jnp.int32)
    source_child = sources // half_rows
    source_maps = jnp.where(
        source_child[:, None] == 0, child_maps[0][None, :], child_maps[1][None, :]
    )
    child_row_index = (
        jnp.arange(child_rows, dtype=jnp.int32)[None, :] * half_rows
        + (sources % half_rows)[:, None]
    )
    mapped_rows = jnp.take_along_axis(source_maps, child_row_index, axis=1)
    dest_rows = mapped_rows % rows_count
    slot_rows = mapped_rows // rows_count
    child_col_index = (
        jnp.arange(child_cols, dtype=jnp.int32)[None, :] * cols_count
        + jnp.arange(cols_count, dtype=jnp.int32)[:, None]
    )
    mapped_cols = child_maps[:, child_col_index]
    dest_cols = mapped_cols % cols_count
    slot_cols = mapped_cols // cols_count
    my_child = row_id // half_rows
    my_order = jnp.where(my_child == 0, child_orders[0], child_orders[1])
    my_rows = child_row_index[row_id]
    my_cols = jnp.arange(child_cols, dtype=jnp.int32) * cols_count + col_id
    offsets = jnp.arange(tile_size, dtype=jnp.int32)[None, :]
    row_keep = (my_rows[:, None] * tile_size + offsets < my_order).astype(jnp.float32)
    col_keep = (my_cols[:, None] * tile_size + offsets < my_order).astype(jnp.float32)
    pieces = pieces * row_keep[:, :, None, None] * col_keep[None, None, :, :]
    capacity = cap_rows * cap_cols
    tile_count = child_rows * child_cols
    source_dest_cols = dest_cols[source_child]
    source_slot_cols = slot_cols[source_child]
    tile_dest = (
        dest_rows[:, None, :, None] * cols_count + source_dest_cols[:, :, None, :]
    ).reshape(rows_count, cols_count, tile_count)
    rank_tiles = earlier_equal(tile_dest)
    send_tiles = (
        one_hot(tile_dest[row_id, col_id], rows_count * cols_count)[:, :, None]
        * one_hot(rank_tiles[row_id, col_id], capacity)[:, None, :]
    )
    flat_pieces = pieces.transpose(0, 2, 1, 3).reshape(tile_count, tile_size, tile_size)
    outgoing = jnp.einsum("fpq,frs->pqrs", send_tiles, flat_pieces, precision=highest)
    incoming = lax.all_to_all(outgoing, ("row", "col"), split_axis=0, concat_axis=0, tiled=True)
    incoming, inverse = lax.optimization_barrier((incoming, inverse))
    arrive_tiles = (tile_dest == row_id * cols_count + col_id).astype(jnp.float32)
    row_slot_flat = jnp.broadcast_to(
        slot_rows[:, None, :, None], (rows_count, cols_count, child_rows, child_cols)
    ).reshape(rows_count, cols_count, tile_count)
    col_slot_flat = jnp.broadcast_to(
        source_slot_cols[:, :, None, :], (rows_count, cols_count, child_rows, child_cols)
    ).reshape(rows_count, cols_count, tile_count)
    placement = jnp.einsum(
        "jlf,jlfa,jlfb,jlfq->abjlq",
        arrive_tiles,
        one_hot(row_slot_flat, row_tiles),
        one_hot(col_slot_flat, col_tiles),
        one_hot(rank_tiles, capacity),
        precision=highest,
    )
    placement = placement.reshape(row_tiles, col_tiles, rows_count * cols_count, capacity)
    added = jnp.einsum("abpq,pqrs->arbs", placement, incoming, precision=highest)
    matrix = matrix + added
    glob_rows = jnp.arange(row_tiles, dtype=jnp.int32) * rows_count + row_id

    panel_cols = lax.all_gather(matrix[0], "row", axis=0)[:panel_tiles]
    panel_cols = panel_cols.reshape(panel_order, col_tiles * tile_size)
    panel_rows = lax.all_gather(matrix[:, :, :lead_cols, :], "col", axis=3)
    panel_rows = panel_rows.reshape(row_tiles * tile_size, lead_cols * cols_count * tile_size)
    panel_rows = panel_rows[:, :panel_order]
    lower_rows = jnp.einsum("rx,yx->ry", panel_rows, inverse, precision=high)
    lower_cols = jnp.einsum("yx,xc->yc", inverse, panel_cols, precision=high)
    lower_tiles = lower_rows.reshape(row_tiles, tile_size, panel_order)
    factor_row = lax.dynamic_slice_in_dim(
        factor, jnp.minimum(row_id, panel_tiles - 1) * tile_size, tile_size, 0
    )
    top = jnp.where(row_id < panel_tiles, factor_row, lower_tiles[0])
    panel = jnp.concatenate([top[None], lower_tiles[1:]], 0)
    columns = []
    for local_col in range(lead_cols):
        column = jnp.minimum(local_col * cols_count + col_id, panel_tiles - 1)
        columns.append(lax.dynamic_slice_in_dim(panel, column * tile_size, tile_size, 2))
    matrix = update(
        jnp.stack([row_id, col_id]).astype(jnp.int32),
        matrix,
        split(lower_tiles, 2, False),
        split(lower_cols, 0, True),
        jnp.stack(columns, 0),
        panel_tiles,
        rows_count,
        cols_count,
    )
    return matrix.reshape(row_tiles, 1, tile_size, col_tiles, 1, tile_size)


def solution(mesh):
    in_specs = (
        P(None, "row", None, None, "col", None),
        P(None, "row", None, None, "col", None),
        P(),
        P(),
    )
    out_specs = P(None, "row", None, None, "col", None)
    return jax.shard_map(shards, mesh=mesh, in_specs=in_specs, out_specs=out_specs, check_vma=False)
```
